32 devices in a mesh: parts: 2 (over y), seq: 4 (over z), head: 4 (over x, core).
Axes of the slice: x: 2, y: 2, z: 4, core: 2. Of those that a mesh axis runs over, the one named last changes fastest.
Arguments:
- queries: bfloat16 [256, 8192], P(('parts', 'seq'), 'head'), parts along dimension 0, may hold values from -110 to 110
- root_keys: bfloat16 [16384, 1024], P(('parts', 'seq'), 'head'), parts along dimension 0, may hold values from -6 to 6
- root_values: bfloat16 [16384, 1024], P(('parts', 'seq'), 'head'), parts along dimension 0, may hold values from -6 to 6
- branch_keys: bfloat16 [16, 2048, 1024], P(('parts', 'seq'), None, 'head'), parts along dimension 0, may hold values from -6 to 6
- branch_values: bfloat16 [16, 2048, 1024], P(('parts', 'seq'), None, 'head'), parts along dimension 0, may hold values from -6 to 6
- branch_id: int32 [256, 1], P('parts'), parts along dimension 0, may hold values from 0 to 7; in each aligned block of 128 rows (0 to 127, 128 to 255, ...) at most 32 rows name the same one
- doc_len: int32 [16], P('parts'), parts along dimension 0, may hold values from 1 to 2048, 10240 in all
Outputs:
- attended: bfloat16 [256, 8192], P(('parts', 'seq'), 'head'), parts along dimension 0
The draws below stay inside these ranges and needn't reach their ends.
There are 2 independent parts, one for each index of `parts`. The reference program is written for one: setup_inputs(seed, part) draws one part's arguments, and reference() takes and returns one part's arrays. A program takes and returns all parts, laid end to end along the dimension named above; each array names one. Nothing has to cross between parts.
Inputs may be any that keep to these rules, and one draw needn't show every extreme that they name: `branch_id`: each of the 8 branches is named by at most 32 rows, a bound that some block reaches. `doc_len`: the 8 lengths of ONE part sum to 10240 and the largest of them is exactly 2048; the printed array holds all parts end to end, so its whole sum is that total times the number of parts.
All inputs are finite; a program needn't handle non-finite values.
Results may differ from the reference program's by a relative error of at most 0.008.
Values may be sent and summed in bfloat16 or wider, within the bound.
A program may use at most 64 MiB of HBM per device.

```python
import math
import jax
import jax.numpy as jnp
import numpy as np
from jax import lax

QHEADS = 64
KVHEADS = 8
HEAD_DIM = 128
BRANCH_LEN = 2048
ROOT = 8192
ROWS = 128
BRANCHES = 8
MOST_ROWS = 32


def draw_queries(key, part):
    extent = (ROWS, QHEADS * HEAD_DIM)
    result = jnp.clip(jax.random.normal(key, extent, jnp.float32), -6.0, 6.0)
    return result.astype(jnp.bfloat16)


def shard_levels(stream_key, dims, cuts, low, high):
    loudness = 1.0
    for axis_at, blocks in cuts:
        steps = jax.random.uniform(jax.random.fold_in(jax.random.fold_in(stream_key, 6), axis_at), (blocks,), jnp.float32, low / len(cuts), high / len(cuts))
        loudness = loudness * jnp.repeat(jnp.exp(steps), dims[axis_at] // blocks).reshape((-1,) + (1,) * (len(dims) - 1 - axis_at))
    return loudness


def profile(amount, total, limit, skew):
    weights = [(1 << 20) // math.isqrt(standing ** skew) + 1 for standing in range(2, amount + 1)]
    surplus, given = total - limit - (amount - 1), [1] * (amount - 1)
    while surplus > 0:
        movable = [i for i in range(amount - 1) if given[i] < limit]
        mass, left = sum([weights[i] for i in movable]), surplus
        for i in movable:
            extra = min(limit - given[i], max(1, left * weights[i] // mass), surplus)
            given[i] = given[i] + extra
            surplus = surplus - extra
    return np.array([limit] + given)


def ragged(rng, amount, total, reach, skew):
    if amount == 2:
        one = jax.random.randint(rng, (), max(1, total - reach), min(reach, total - 1) + 1)
        return jnp.stack([one, total - one])
    tallies = jnp.asarray(profile(amount, total, reach, skew), jnp.int32)
    twos = (amount - 1) // 2
    giver, sink = tallies[1:1 + 2 * twos:2], tallies[2:2 + 2 * twos:2]
    slack = jnp.minimum(giver - 1, reach - sink)
    shifted = jax.random.randint(jax.random.fold_in(rng, 1), (twos,), 0, 1 << 20) % (slack + 1)
    tallies = tallies.at[1:1 + 2 * twos:2].set(giver - shifted).at[2:2 + 2 * twos:2].set(sink + shifted)
    return tallies[jax.random.permutation(jax.random.fold_in(rng, 2), amount)]


def assign_block(stream_key, own, number, rows, number_of, top, most, slope):
    sequence = jax.random.permutation(stream_key, number_of)
    heavy_load, ordinary = portions_of(number_of, rows * top, most, slope, True), portions_of(number_of, rows * top, most, slope, False)
    places = jnp.arange(number_of)

    def named(sizes, rotation):
        used = int((sizes > 0).sum())
        fixed = max(1, used // 4)
        shifted = fixed + (places - fixed + rotation * (used - fixed)) % max(1, number_of - fixed)
        return jnp.zeros((number_of,), jnp.int32).at[sequence[jnp.where(places < fixed, places, shifted)]].set(jnp.asarray(sizes, jnp.int32))

    sizes = jnp.where(number % 4 == 0, named(heavy_load, number // 4), named(ordinary, number - number // 4 - 1))
    mixed = jax.random.permutation(jax.random.fold_in(own, 3), number_of)
    giver, receiver = mixed[0:number_of // 2 * 2:2], mixed[1:number_of // 2 * 2:2]
    room = jnp.minimum(sizes[giver] - 1, most - sizes[receiver]) // 2
    room = jnp.where((giver == sequence[0]) | (receiver == sequence[0]) | (sizes[receiver] == 0), 0, jnp.maximum(room, 0))
    shifted = jax.random.randint(jax.random.fold_in(own, 4), (number_of // 2,), 0, 1 << 20) % (room + 1)
    sizes = sizes.at[giver].add(-shifted).at[receiver].add(shifted)
    members = jnp.searchsorted(jnp.cumsum(sizes), jnp.arange(rows * top), side="right").astype(jnp.int32)
    grid = members.reshape(top, rows).T
    grid = grid[jax.random.permutation(jax.random.fold_in(own, 1), rows)]
    rotation = jax.random.randint(jax.random.fold_in(own, 2), (rows, 1), 0, top)
    return jnp.take_along_axis(grid, (jnp.arange(top)[None, :] + rotation) % top, axis=1)


def portions_of(amount, total, reach, lean, full):
    portions = [(1 << 20) // math.isqrt(grade ** lean) + 1 for grade in range(1, amount + 1)]
    largest = reach if full else min(reach, max(-(-total // amount), total * portions[0] // sum(portions)))
    least = 1 if total - largest >= amount - 1 else 0
    given, surplus = [largest] + [least] * (amount - 1), total - largest - least * (amount - 1)
    while surplus > 0:
        movable = [i for i in range(1, amount) if given[i] < largest] or [i for i in range(1, amount) if given[i] < reach]
        mass, budget = sum([portions[i] for i in movable]), surplus
        for i in movable:
            extra = min(reach - given[i], max(1, budget * portions[i] // mass), surplus)
            given[i] = given[i] + extra
            surplus = surplus - extra
    return np.array(given)


def centred(rng, dims, scale, reach, cuts=(), kind=jnp.bfloat16):
    level = shard_levels(rng, dims, cuts, -0.22, 0.18) if cuts else 1.0
    values = jax.random.normal(rng, dims, jnp.float32) * scale * level
    return jnp.minimum(jnp.maximum(values, -reach), reach).astype(kind)


def setup_inputs(seed: int = 0, part: int = 0) -> dict:
    keys = jax.random.split(jax.random.key(seed), 8)
    part_keys = jax.random.split(jax.random.fold_in(keys[7], part), 8)
    queries = draw_queries(jax.random.fold_in(jax.random.fold_in(keys[7], part), 71), part)
    root_keys = centred(part_keys[1], (ROOT, KVHEADS * HEAD_DIM), 1.0, 6.0, ((0, 4), (1, 4)))
    root_values = centred(part_keys[2], (ROOT, KVHEADS * HEAD_DIM), 1.0, 6.0, ((0, 4), (1, 4)))
    branch_keys = centred(part_keys[3], (BRANCHES, BRANCH_LEN, KVHEADS * HEAD_DIM), 1.0, 6.0, ((0, 4), (2, 4)))
    branch_values = centred(part_keys[4], (BRANCHES, BRANCH_LEN, KVHEADS * HEAD_DIM), 1.0, 6.0, ((0, 4), (2, 4)))
    branch_id_keys = jax.random.split(jax.random.fold_in(part_keys[5], 1), ROWS // ROWS)
    branch_id_turns = jax.random.permutation(jax.random.fold_in(part_keys[5], 3), ROWS // ROWS)
    branch_id = jax.vmap(lambda own, number: assign_block(jax.random.fold_in(part_keys[5], 2), own, number, ROWS, BRANCHES, 1, MOST_ROWS, 2))(branch_id_keys, branch_id_turns).reshape((ROWS, 1))
    doc_len = ragged(part_keys[6], BRANCHES, BRANCHES * BRANCH_LEN * 5 // 8, BRANCH_LEN, 2).astype(jnp.int32)
    return {"queries": queries, "root_keys": root_keys, "root_values": root_values, "branch_keys": branch_keys, "branch_values": branch_values, "branch_id": branch_id, "doc_len": doc_len}


masked_score = -1.0e30


def attend(query_head_rows, key_tile_rows, value_tile_rows, usable):
    logit_scale = HEAD_DIM ** -0.5
    logit_scores = jnp.einsum('mfsa,nfa->mfsn', query_head_rows.astype(jnp.float32), key_tile_rows.astype(jnp.float32)) * logit_scale
    keep = usable[:, None, None, :]
    logit_scores = jnp.where(keep, logit_scores, masked_score)
    row_max = jnp.max(logit_scores, axis=-1)
    softmax_weights = jnp.where(keep, jnp.exp(logit_scores - row_max[..., None]), 0.0)
    row_sum = jnp.sum(softmax_weights, axis=-1)
    weighted_values = jnp.einsum('taoz,zah->taoh', softmax_weights.astype(jnp.bfloat16).astype(jnp.float32), value_tile_rows.astype(jnp.float32))
    return row_max, row_sum, weighted_values


def combine(first, second):
    row_max = jnp.maximum(first[0], second[0])
    factor_a = jnp.exp(first[0] - row_max)
    factor_b = jnp.exp(second[0] - row_max)
    return (row_max, first[1] * factor_a + second[1] * factor_b,
            first[2] * factor_a[..., None] + second[2] * factor_b[..., None])


def reference(queries, root_keys, root_values, branch_keys, branch_values, branch_id, doc_len):
    group = QHEADS // KVHEADS
    query_head_rows = queries.reshape(ROWS, KVHEADS, group, HEAD_DIM)
    block_len = min(1024, ROOT)
    key_blocks = root_keys.reshape(ROOT // block_len, block_len, KVHEADS, HEAD_DIM)
    value_blocks = root_values.reshape(ROOT // block_len, block_len, KVHEADS, HEAD_DIM)
    starts = (jnp.full((ROWS, KVHEADS, group), masked_score, jnp.float32),
              jnp.zeros((ROWS, KVHEADS, group), jnp.float32),
              jnp.zeros((ROWS, KVHEADS, group, HEAD_DIM), jnp.float32))

    def root_step(carry, pair):
        usable = jnp.ones((1, block_len), bool)
        return combine(carry, attend(query_head_rows, pair[0], pair[1], usable)), None

    root_part, _ = lax.scan(root_step, starts, (key_blocks, value_blocks))

    def one_branch(branch):
        chosen = jnp.argsort((branch_id[:, 0] != branch).astype(jnp.int32), stable=True)[:MOST_ROWS].astype(jnp.int32)
        row_live = branch_id[chosen, 0] == branch
        key_live = jnp.arange(BRANCH_LEN) < doc_len[branch]
        usable = row_live[:, None] & key_live[None, :]
        key_tile_rows = lax.dynamic_index_in_dim(branch_keys, branch, 0, keepdims=False).reshape(BRANCH_LEN, KVHEADS, HEAD_DIM)
        value_tile_rows = lax.dynamic_index_in_dim(branch_values, branch, 0, keepdims=False).reshape(BRANCH_LEN, KVHEADS, HEAD_DIM)
        result = attend(query_head_rows[chosen], key_tile_rows, value_tile_rows, usable)
        target = jnp.where(row_live, chosen, ROWS).astype(jnp.int32)
        return result + (target,)

    mapped = lax.map(one_branch, jnp.arange(BRANCHES, dtype=jnp.int32))
    targets = mapped[3].reshape(-1)
    branch_part = (
        starts[0].at[targets].set(mapped[0].reshape(-1, KVHEADS, group), mode="drop"),
        starts[1].at[targets].set(mapped[1].reshape(-1, KVHEADS, group), mode="drop"),
        starts[2].at[targets].set(mapped[2].reshape(-1, KVHEADS, group, HEAD_DIM), mode="drop"))
    joined = combine(root_part, branch_part)
    attended = joined[2] / joined[1][..., None]
    return attended.astype(jnp.bfloat16).reshape(ROWS, QHEADS * HEAD_DIM)
```

```python
import functools

import jax
import jax.numpy as jnp
from jax import lax
from jax.experimental import pallas as pl
from jax.experimental.pallas import tpu as pltpu
from jax.sharding import PartitionSpec as P

QHEADS = 64
KVHEADS = 8
HEAD_DIM = 128
GROUP = QHEADS // KVHEADS
MESH = pl.DeviceIdType.MESH
LOG2E = 1.4426950408889634
SCALE2 = HEAD_DIM ** (-0.5) * LOG2E
MASKED = -1e30


def attend(q, keys, values, live=None):
    s = lax.dot_general(q, keys, (((1,), (1,)), ((), ())), preferred_element_type=jnp.float32)
    if live is not None:
        s = jnp.where(live, s, MASKED)
    m = jnp.max(s, axis=1, keepdims=True)
    p = jnp.exp2((s - m) * SCALE2).astype(jnp.bfloat16)
    o = jnp.dot(p, values, preferred_element_type=jnp.float32)
    return m, o


def stack_heads(rows):
    return jnp.concatenate(
        [rows[:, h * HEAD_DIM : (h + 1) * HEAD_DIM] for h in range(GROUP)], axis=0
    )


def kernel(
    n,
    kv,
    q_hbm,
    rk_hbm,
    rv_hbm,
    bk_hbm,
    bv_hbm,
    id_ref,
    len_ref,
    out_ref,
    qg,
    rk,
    rv,
    bk,
    bv,
    root_o,
    root_m,
    root_l,
    branch_o,
    part_o,
    part_s,
    recv_o,
    recv_s,
    own_sem,
    load_sem,
    qsend_sem,
    qrecv_sem,
    osend_sem,
    orecv_sem,
    ssend_sem,
    srecv_sem,
):
    me = lax.axis_index("seq")
    rows = q_hbm.shape[0]
    all_rows = n * rows
    width = GROUP * HEAD_DIM
    branches = bk_hbm.shape[0]
    branch_len = bk_hbm.shape[1]
    most = 2 * rows // branches
    slots = branches * most

    barrier = pltpu.get_barrier_semaphore()
    for k in range(1, n):
        pl.semaphore_signal(
            barrier, inc=1, device_id={"seq": lax.rem(me + k, n)}, device_id_type=MESH
        )

    def head_cols(f):
        return pl.ds(f * HEAD_DIM, HEAD_DIM)

    def shard_rows(s):
        return pl.ds(pl.multiple_of(s * rows, rows), rows)

    own, loads_k, loads_v = [], [], []
    for f in range(kv):
        own.append(
            pltpu.make_async_copy(
                q_hbm.at[:, pl.ds(f * width, width)], qg.at[f, shard_rows(me)], own_sem.at[f]
            )
        )
        loads_k.append(pltpu.make_async_copy(rk_hbm.at[:, head_cols(f)], rk.at[f], load_sem.at[0, f, 0]))
        loads_v.append(
            pltpu.make_async_copy(
                rv_hbm.at[:, head_cols(f)], rv.at[f, :, pl.ds(0, HEAD_DIM)], load_sem.at[1, f, 0]
            )
        )
    bloads_k, bloads_v = [], []
    for f in range(kv):
        bloads_k.append(
            [
                pltpu.make_async_copy(
                    bk_hbm.at[b, :, head_cols(f)], bk.at[f, b], load_sem.at[2, f, b]
                )
                for b in range(branches)
            ]
        )
        bloads_v.append(
            [
                pltpu.make_async_copy(
                    bv_hbm.at[b, :, head_cols(f)],
                    bv.at[f, b, :, pl.ds(0, HEAD_DIM)],
                    load_sem.at[3, f, b],
                )
                for b in range(branches)
            ]
        )
    for f in range(kv):
        own[f].start()
    loads_k[0].start()

    pl.semaphore_wait(barrier, n - 1)

    def q_copy(f, s, way, hop, src):
        to = me + 1 if way == 0 else me - 1
        return pltpu.make_async_remote_copy(
            src_ref=src,
            dst_ref=qg.at[f, shard_rows(s)],
            send_sem=qsend_sem.at[f, way, hop],
            recv_sem=qrecv_sem.at[f, s],
            device_id={"seq": to},
            device_id_type=MESH,
        )

    def send_own(f):
        src = q_hbm.at[:, pl.ds(f * width, width)]

        @pl.when(me < n - 1)
        def _():
            q_copy(f, me, 0, 0, src).start()

        @pl.when(me > 0)
        def _():
            q_copy(f, me, 1, 0, src).start()

    def forward(f, hop):
        left, right = me - hop, me + hop

        @pl.when(left >= 0)
        def _():
            block = qg.at[f, shard_rows(left)]
            q_copy(f, left, 0, hop, block).wait_recv()

            @pl.when(me < n - 1)
            def _():
                q_copy(f, left, 0, hop, block).start()

        @pl.when(right < n)
        def _():
            block = qg.at[f, shard_rows(right)]
            q_copy(f, right, 1, hop, block).wait_recv()

            @pl.when(me > 0)
            def _():
                q_copy(f, right, 1, hop, block).start()

    def sent(f, hop):
        left, right = me - hop, me + hop

        @pl.when((left >= 0) & (me < n - 1))
        def _():
            q_copy(f, left, 0, hop, qg.at[f, shard_rows(left)]).wait_send()

        @pl.when((right < n) & (me > 0))
        def _():
            q_copy(f, right, 1, hop, qg.at[f, shard_rows(right)]).wait_send()

    for f in range(kv):
        send_own(f)

    for f in range(kv):
        rv[f, :, HEAD_DIM:] = jnp.ones((rv.shape[1], HEAD_DIM), jnp.bfloat16)
        for b in range(branches):
            bv[f, b, :, HEAD_DIM:] = jnp.ones((branch_len, HEAD_DIM), jnp.bfloat16)
    for f in range(kv):
        if f:
            loads_k[f].start()
        loads_v[f].start()
        for b in range(branches):
            bloads_k[f][b].start()
            bloads_v[f][b].start()

    slot = lax.broadcasted_iota(jnp.int32, (all_rows, slots), 1)
    named = id_ref[...] == me * branches + slot // most
    named_b = jnp.where(named, 1.0, 0.0).astype(jnp.bfloat16)
    tri = jnp.where(
        lax.broadcasted_iota(jnp.int32, (all_rows, all_rows), 0)
        >= lax.broadcasted_iota(jnp.int32, (all_rows, all_rows), 1),
        1.0,
        0.0,
    ).astype(jnp.bfloat16)
    rank = jnp.dot(tri, named_b, preferred_element_type=jnp.float32)
    place = named & (rank == (lax.rem(slot, most) + 1).astype(jnp.float32))
    place_f = jnp.where(place, 1.0, 0.0)
    place_b = place_f.astype(jnp.bfloat16)
    held = jnp.dot(place_b, jnp.ones((slots, HEAD_DIM), jnp.bfloat16), preferred_element_type=jnp.float32)

    lane = lax.broadcasted_iota(jnp.int32, (rows, HEAD_DIM), 1)
    slot_lane = lax.broadcasted_iota(jnp.int32, (most, HEAD_DIM), 1)
    position = lax.broadcasted_iota(jnp.int32, (1, branch_len), 1)

    def o_copy(f, s, src_dev):
        return pltpu.make_async_remote_copy(
            src_ref=part_o.at[f, s],
            dst_ref=recv_o.at[f, src_dev],
            send_sem=osend_sem.at[f, s],
            recv_sem=orecv_sem.at[f, src_dev],
            device_id={"seq": s},
            device_id_type=MESH,
        )

    def s_copy(f, s, src_dev):
        return pltpu.make_async_remote_copy(
            src_ref=part_s.at[f, s],
            dst_ref=recv_s.at[f, src_dev],
            send_sem=ssend_sem.at[f, s],
            recv_sem=srecv_sem.at[f, src_dev],
            device_id={"seq": s},
            device_id_type=MESH,
        )

    own[0].wait()
    for hop in range(1, n):
        forward(0, hop)
    loads_k[0].wait()
    loads_v[0].wait()

    for f in range(kv):
        if f:
            loads_k[f].wait()
            loads_v[f].wait()

        def root_step(s, carry, f=f):
            m, o = attend(stack_heads(qg[f, shard_rows(s)]), rk[f], rv[f])
            ms = jnp.zeros((rows, HEAD_DIM), jnp.float32)
            ls = jnp.ones((rows, HEAD_DIM), jnp.float32)
            for h in range(GROUP):
                part = slice(h * rows, (h + 1) * rows)
                root_o[shard_rows(s), h * HEAD_DIM : (h + 1) * HEAD_DIM] = o[part, :HEAD_DIM]
                ms = jnp.where(lane == h, m[part], ms)
                ls = jnp.where(lane == h, o[part, HEAD_DIM:], ls)
            root_m[shard_rows(s)] = ms
            root_l[shard_rows(s)] = ls
            if f + 1 < kv:

                @pl.when(s > 0)
                def _():
                    forward(f + 1, s)

            return carry

        lax.fori_loop(0, n, root_step, 0)
        if f + 1 < kv:
            own[f + 1].wait()

        picked = lax.dot_general(
            place_b, qg[f], (((0,), (0,)), ((), ())), preferred_element_type=jnp.float32
        ).astype(jnp.bfloat16)
        lses = []
        for b in range(branches):
            bloads_k[f][b].wait()
            bloads_v[f][b].wait()
            live = position < len_ref[me * branches + b]
            m, o = attend(
                stack_heads(picked[b * most : (b + 1) * most]), bk[f, b], bv[f, b], live
            )
            ms = jnp.zeros((most, HEAD_DIM), jnp.float32)
            ls = jnp.ones((most, HEAD_DIM), jnp.float32)
            for h in range(GROUP):
                part = slice(h * most, (h + 1) * most)
                branch_o[b * most : (b + 1) * most, h * HEAD_DIM : (h + 1) * HEAD_DIM] = (
                    o[part, :HEAD_DIM] / o[part, HEAD_DIM:]
                ).astype(jnp.bfloat16)
                ms = jnp.where(slot_lane == h, m[part], ms)
                ls = jnp.where(slot_lane == h, o[part, HEAD_DIM:], ls)
            lses.append(ms * SCALE2 + jnp.log2(ls))
        put_s = jnp.dot(
            place_f,
            jnp.concatenate(lses, axis=0),
            precision=lax.Precision.HIGHEST,
            preferred_element_type=jnp.float32,
        )
        put_s = jnp.where(held > 0.5, put_s, MASKED)
        root_sum = root_l[...]
        root_lse = root_m[...] * SCALE2 + jnp.log2(root_sum)
        top = jnp.maximum(root_lse, put_s)
        root_w = jnp.exp2(root_lse - top)
        branch_w = jnp.exp2(put_s - top)
        total = root_w + branch_w
        joined = top + jnp.log2(total)
        root_m[...] = root_w / (total * root_sum)
        root_l[...] = branch_w / total
        for s in range(n):
            part_s[f, s] = joined[s * rows : (s + 1) * rows]
        put_o = jnp.dot(place_b, branch_o[...], preferred_element_type=jnp.float32)
        for h in range(GROUP):
            cols = slice(h * HEAD_DIM, (h + 1) * HEAD_DIM)
            mixed = (
                root_o[:, cols] * root_m[:, h : h + 1] + put_o[:, cols] * root_l[:, h : h + 1]
            ).astype(jnp.bfloat16)
            for s in range(n):
                part_o[f, s, :, cols] = mixed[s * rows : (s + 1) * rows]
        for k in range(1, n):
            s = lax.rem(me + k, n)
            o_copy(f, s, me).start()
            s_copy(f, s, me).start()
    for f in range(kv):
        for k in range(1, n):
            s = lax.rem(me + k, n)
            o_copy(f, s, s).wait_recv()
            s_copy(f, s, s).wait_recv()
        recv_s[f, me] = part_s[f, me]
        recv_o[f, me] = part_o[f, me]
        lse = [recv_s[f, s] for s in range(n)]
        top = functools.reduce(jnp.maximum, lse)
        weights = [jnp.exp2(x - top) for x in lse]
        total = functools.reduce(jnp.add, weights)
        coefs = [w / total for w in weights]
        for h in range(GROUP):
            cols = slice(h * HEAD_DIM, (h + 1) * HEAD_DIM)
            acc = recv_o[f, 0, :, cols].astype(jnp.float32) * coefs[0][:, h : h + 1]
            for s in range(1, n):
                acc += recv_o[f, s, :, cols].astype(jnp.float32) * coefs[s][:, h : h + 1]
            out_ref[:, f * width + h * HEAD_DIM : f * width + (h + 1) * HEAD_DIM] = acc.astype(
                jnp.bfloat16
            )

    for f in range(kv):
        for hop in range(n - 1):
            sent(f, hop)
        for k in range(1, n):
            s = lax.rem(me + k, n)
            o_copy(f, s, me).wait_send()
            s_copy(f, s, me).wait_send()


def body(n, queries, root_keys, root_values, branch_keys, branch_values, branch_id, doc_len):
    rows = queries.shape[0]
    kv = root_keys.shape[1] // HEAD_DIM
    root_len = root_keys.shape[0]
    branches, branch_len = branch_keys.shape[:2]
    width = GROUP * HEAD_DIM
    all_rows = n * rows
    most = 2 * rows // branches
    slots = branches * most
    any_spec = pl.BlockSpec(memory_space=pl.ANY)
    bf16, f32 = jnp.bfloat16, jnp.float32
    dma = pltpu.SemaphoreType.DMA
    return pl.pallas_call(
        functools.partial(kernel, n, kv),
        out_shape=jax.ShapeDtypeStruct(queries.shape, bf16),
        in_specs=[any_spec] * 5
        + [pl.BlockSpec(memory_space=pltpu.VMEM), pl.BlockSpec(memory_space=pltpu.SMEM)],
        out_specs=pl.BlockSpec(memory_space=pltpu.VMEM),
        scratch_shapes=[
            pltpu.VMEM((kv, all_rows, width), bf16),
            pltpu.VMEM((kv, root_len, HEAD_DIM), bf16),
            pltpu.VMEM((kv, root_len, 2 * HEAD_DIM), bf16),
            pltpu.VMEM((kv, branches, branch_len, HEAD_DIM), bf16),
            pltpu.VMEM((kv, branches, branch_len, 2 * HEAD_DIM), bf16),
            pltpu.VMEM((all_rows, width), f32),
            pltpu.VMEM((all_rows, HEAD_DIM), f32),
            pltpu.VMEM((all_rows, HEAD_DIM), f32),
            pltpu.VMEM((slots, width), bf16),
            pltpu.VMEM((kv, n, rows, width), bf16),
            pltpu.VMEM((kv, n, rows, HEAD_DIM), f32),
            pltpu.VMEM((kv, n, rows, width), bf16),
            pltpu.VMEM((kv, n, rows, HEAD_DIM), f32),
            dma((kv,)),
            dma((4, kv, branches)),
            dma((kv, 2, n)),
            dma((kv, n)),
            dma((kv, n)),
            dma((kv, n)),
            dma((kv, n)),
            dma((kv, n)),
        ],
        compiler_params=pltpu.CompilerParams(
            collective_id=0, has_side_effects=True, vmem_limit_bytes=60 * 1024 * 1024
        ),
    )(queries, root_keys, root_values, branch_keys, branch_values, branch_id, doc_len)


def solution(mesh):
    in_specs = (
        P(("parts", "seq"), "head"),
        P(("parts", "seq"), "head"),
        P(("parts", "seq"), "head"),
        P(("parts", "seq"), None, "head"),
        P(("parts", "seq"), None, "head"),
        P("parts", None),
        P("parts"),
    )
    out_specs = P(("parts", "seq"), "head")
    return jax.shard_map(
        functools.partial(body, mesh.shape["seq"]),
        mesh=mesh,
        in_specs=in_specs,
        out_specs=out_specs,
        check_vma=False,
    )
```

```python
import functools

import jax
import jax.numpy as jnp
from jax import lax
from jax.experimental import pallas as pl
from jax.experimental.pallas import tpu as pltpu
from jax.sharding import PartitionSpec as P

QHEADS = 64
KVHEADS = 8
HEAD_DIM = 128
GROUP = QHEADS // KVHEADS
MESH = pl.DeviceIdType.MESH
LOG2E = 1.4426950408889634
SCALE2 = HEAD_DIM ** (-0.5) * LOG2E
MASKED = -1e30


def attend(q, keys, values, live=None):
    s = lax.dot_general(q, keys, (((1,), (1,)), ((), ())), preferred_element_type=jnp.float32)
    if live is not None:
        s = jnp.where(live, s, MASKED)
    m = jnp.max(s, axis=1, keepdims=True)
    p = jnp.exp2((s - m) * SCALE2).astype(jnp.bfloat16)
    o = jnp.dot(p, values, preferred_element_type=jnp.float32)
    return m, o


def stack_heads(rows):
    return jnp.concatenate(
        [rows[:, h * HEAD_DIM : (h + 1) * HEAD_DIM] for h in range(GROUP)], axis=0
    )


def kernel(
    n,
    kv,
    q_hbm,
    rk_hbm,
    rv_hbm,
    bk_hbm,
    bv_hbm,
    id_ref,
    len_ref,
    out_ref,
    qg,
    rk,
    rv,
    bk,
    bv,
    root_o,
    root_m,
    root_l,
    branch_o,
    part,
    recv,
    own_sem,
    load_sem,
    qsend_sem,
    qrecv_sem,
    psend_sem,
    precv_sem,
):
    me = lax.axis_index("seq")
    rows = q_hbm.shape[0]
    all_rows = n * rows
    width = GROUP * HEAD_DIM
    branches = bk_hbm.shape[0]
    branch_len = bk_hbm.shape[1]
    most = 2 * rows // branches
    slots = branches * most
    has_left, has_right = me > 0, me < n - 1

    barrier = pltpu.get_barrier_semaphore()

    @pl.when(has_left)
    def _():
        pl.semaphore_signal(barrier, inc=1, device_id={"seq": me - 1}, device_id_type=MESH)

    @pl.when(has_right)
    def _():
        pl.semaphore_signal(barrier, inc=1, device_id={"seq": me + 1}, device_id_type=MESH)

    def head_cols(f):
        return pl.ds(f * HEAD_DIM, HEAD_DIM)

    def shard_rows(s):
        return pl.ds(pl.multiple_of(s * rows, rows), rows)

    own, loads_k, loads_v = [], [], []
    for f in range(kv):
        own.append(
            pltpu.make_async_copy(
                q_hbm.at[:, pl.ds(f * width, width)], qg.at[f, shard_rows(me)], own_sem.at[f]
            )
        )
        loads_k.append(
            pltpu.make_async_copy(rk_hbm.at[:, head_cols(f)], rk.at[f], load_sem.at[0, f, 0])
        )
        loads_v.append(
            pltpu.make_async_copy(
                rv_hbm.at[:, head_cols(f)], rv.at[f, :, pl.ds(0, HEAD_DIM)], load_sem.at[1, f, 0]
            )
        )
    bloads_k, bloads_v = [], []
    for f in range(kv):
        bloads_k.append(
            [
                pltpu.make_async_copy(
                    bk_hbm.at[b, :, head_cols(f)], bk.at[f, b], load_sem.at[2, f, b]
                )
                for b in range(branches)
            ]
        )
        bloads_v.append(
            [
                pltpu.make_async_copy(
                    bv_hbm.at[b, :, head_cols(f)],
                    bv.at[f, b, :, pl.ds(0, HEAD_DIM)],
                    load_sem.at[3, f, b],
                )
                for b in range(branches)
            ]
        )
    own[0].start()
    loads_k[0].start()

    for f in range(kv):
        rv[f, :, HEAD_DIM:] = jnp.ones((rv.shape[1], HEAD_DIM), jnp.bfloat16)
        loads_v[f].start()
        if f:
            loads_k[f].start()
            own[f].start()
        for b in range(branches):
            bv[f, b, :, HEAD_DIM:] = jnp.ones((branch_len, HEAD_DIM), jnp.bfloat16)
            bloads_k[f][b].start()
            bloads_v[f][b].start()

    pl.semaphore_wait(barrier, jnp.where(has_left & has_right, 2, 1))

    def q_copy(f, s, way, hop, src):
        return pltpu.make_async_remote_copy(
            src_ref=src,
            dst_ref=qg.at[f, shard_rows(s)],
            send_sem=qsend_sem.at[f, way, hop],
            recv_sem=qrecv_sem.at[f, s],
            device_id={"seq": me + 1 if way == 0 else me - 1},
            device_id_type=MESH,
        )

    def send_own(f):
        src = q_hbm.at[:, pl.ds(f * width, width)]

        @pl.when(has_right)
        def _():
            q_copy(f, me, 0, 0, src).start()

        @pl.when(has_left)
        def _():
            q_copy(f, me, 1, 0, src).start()

    def pass_right(f, hop):
        s = me - hop
        block = qg.at[f, shard_rows(s)]
        q_copy(f, s, 0, hop, block).wait_recv()

        @pl.when(has_right)
        def _():
            q_copy(f, s, 0, hop, block).start()

    def pass_left(f, hop):
        s = me + hop
        block = qg.at[f, shard_rows(s)]
        q_copy(f, s, 1, hop, block).wait_recv()

        @pl.when(has_left)
        def _():
            q_copy(f, s, 1, hop, block).start()

    def forward(f, hop):
        @pl.when(me - hop >= 0)
        def _():
            pass_right(f, hop)

        @pl.when(me + hop < n)
        def _():
            pass_left(f, hop)

    def sent(f, hop):
        left, right = me - hop, me + hop

        @pl.when((left >= 0) & has_right)
        def _():
            q_copy(f, left, 0, hop, qg.at[f, shard_rows(left)]).wait_send()

        @pl.when((right < n) & has_left)
        def _():
            q_copy(f, right, 1, hop, qg.at[f, shard_rows(right)]).wait_send()

    send_own(0)

    slot = lax.broadcasted_iota(jnp.int32, (slots, all_rows), 0)
    named = id_ref[...] == me * branches + slot // most
    named_b = jnp.where(named, 1.0, 0.0).astype(jnp.bfloat16)
    tri = jnp.where(
        lax.broadcasted_iota(jnp.int32, (all_rows, all_rows), 0)
        <= lax.broadcasted_iota(jnp.int32, (all_rows, all_rows), 1),
        1.0,
        0.0,
    ).astype(jnp.bfloat16)
    rank = jnp.dot(named_b, tri, preferred_element_type=jnp.float32)
    pick_f = jnp.where(named & (rank == (lax.rem(slot, most) + 1).astype(jnp.float32)), 1.0, 0.0)
    pick_b = pick_f.astype(jnp.bfloat16)
    place_f = pick_f.T
    place_b = place_f.astype(jnp.bfloat16)
    held = jnp.dot(
        place_b, jnp.ones((slots, HEAD_DIM), jnp.bfloat16), preferred_element_type=jnp.float32
    )

    lane = lax.broadcasted_iota(jnp.int32, (rows, HEAD_DIM), 1)
    all_lane = lax.broadcasted_iota(jnp.int32, (all_rows, HEAD_DIM), 1)
    slot_lane = lax.broadcasted_iota(jnp.int32, (most, HEAD_DIM), 1)
    position = lax.broadcasted_iota(jnp.int32, (1, branch_len), 1)
    side_cols = slice(width, width + HEAD_DIM)

    def split(x, lanes):
        high = x.astype(jnp.bfloat16).astype(jnp.float32)
        rest = x - high
        mid = rest.astype(jnp.bfloat16).astype(jnp.float32)
        low = rest - mid
        return jnp.where(
            lanes < GROUP,
            high,
            jnp.where(
                lanes < 2 * GROUP, pltpu.roll(mid, GROUP, axis=1), pltpu.roll(low, 2 * GROUP, axis=1)
            ),
        ).astype(jnp.bfloat16)

    def whole(x):
        x = x.astype(jnp.float32)
        return (
            x
            + pltpu.roll(x, HEAD_DIM - GROUP, axis=1)
            + pltpu.roll(x, HEAD_DIM - 2 * GROUP, axis=1)
        )

    def merge(f, d, side):
        lse_a = whole(part[f, d, :, side_cols])
        lse_b = whole(recv[f, d, side, :, side_cols])
        top = jnp.maximum(lse_a, lse_b)
        a, b = jnp.exp2(lse_a - top), jnp.exp2(lse_b - top)
        total = a + b
        a, b = a / total, b / total
        for h in range(GROUP):
            cols = slice(h * HEAD_DIM, (h + 1) * HEAD_DIM)
            part[f, d, :, cols] = (
                part[f, d, :, cols].astype(jnp.float32) * a[:, h : h + 1]
                + recv[f, d, side, :, cols].astype(jnp.float32) * b[:, h : h + 1]
            ).astype(jnp.bfloat16)
        part[f, d, :, side_cols] = split(top + jnp.log2(total), lane)

    def p_copy(f, d, side):
        return pltpu.make_async_remote_copy(
            src_ref=part.at[f, d],
            dst_ref=recv.at[f, d, side],
            send_sem=psend_sem.at[f, d],
            recv_sem=precv_sem.at[f, d, side],
            device_id={"seq": me + 1 if side == 0 else me - 1},
            device_id_type=MESH,
        )

    def stage(f, h):
        for side in range(2):

            @pl.when((me if side == 0 else n - 1 - me) == h)
            def _(side=side):
                def one(i, carry):
                    d = n - 1 - i if side == 0 else i

                    @pl.when(h > 0)
                    def _():
                        p_copy(f, d, side).wait_recv()
                        merge(f, d, side)

                    p_copy(f, d, side).start()
                    return carry

                lax.fori_loop(0, n - 1 - h, one, 0)

    def finish(f):
        for side in range(2):

            @pl.when(has_left if side == 0 else has_right)
            def _(side=side):
                p_copy(f, me, side).wait_recv()
                merge(f, me, side)

        out_ref[:, f * width : (f + 1) * width] = part[f, me, :, :width]

    def root(f, s):
        m, o = attend(stack_heads(qg[f, shard_rows(s)]), rk[f], rv[f])
        ms = jnp.zeros((rows, HEAD_DIM), jnp.float32)
        ls = jnp.ones((rows, HEAD_DIM), jnp.float32)
        for h in range(GROUP):
            block = slice(h * rows, (h + 1) * rows)
            root_o[shard_rows(s), h * HEAD_DIM : (h + 1) * HEAD_DIM] = o[block, :HEAD_DIM]
            ms = jnp.where(lane == h, m[block], ms)
            ls = jnp.where(lane == h, o[block, HEAD_DIM:], ls)
        root_m[shard_rows(s)] = ms
        root_l[shard_rows(s)] = ls

    own[0].wait()
    loads_k[0].wait()
    loads_v[0].wait()

    for f in range(kv):
        if f == 0:

            def first_step(j, carry):
                hop, left = (j + 1) // 2, lax.rem(j, 2) == 1
                s = jnp.where(left, me - hop, me + hop)

                @pl.when(left & (s >= 0))
                def _():
                    pass_right(0, hop)

                @pl.when((j > 0) & jnp.logical_not(left) & (s < n))
                def _():
                    pass_left(0, hop)

                if kv > 1:

                    @pl.when(j == 2)
                    def _():
                        send_own(1)

                    @pl.when((j > 2) & jnp.logical_not(left))
                    def _():
                        forward(1, hop - 1)

                @pl.when((s >= 0) & (s < n))
                def _():
                    root(0, s)

                return carry

            lax.fori_loop(0, 2 * n - 1, first_step, 0)
        else:
            own[f].wait()
            loads_k[f].wait()
            loads_v[f].wait()

            def root_step(s, carry, f=f):
                root(f, s)

                @pl.when(s == n - 2)
                def _():
                    stage(f - 1, 1)

                return carry

            lax.fori_loop(0, n, root_step, 0)

        picked = jnp.dot(pick_b, qg[f], preferred_element_type=jnp.float32).astype(jnp.bfloat16)
        lses = []
        for b in range(branches):
            bloads_k[f][b].wait()
            bloads_v[f][b].wait()
            live = position < len_ref[me * branches + b]
            m, o = attend(
                stack_heads(picked[b * most : (b + 1) * most]), bk[f, b], bv[f, b], live
            )
            ms = jnp.zeros((most, HEAD_DIM), jnp.float32)
            ls = jnp.ones((most, HEAD_DIM), jnp.float32)
            for h in range(GROUP):
                block = slice(h * most, (h + 1) * most)
                branch_o[b * most : (b + 1) * most, h * HEAD_DIM : (h + 1) * HEAD_DIM] = (
                    o[block, :HEAD_DIM] / o[block, HEAD_DIM:]
                ).astype(jnp.bfloat16)
                ms = jnp.where(slot_lane == h, m[block], ms)
                ls = jnp.where(slot_lane == h, o[block, HEAD_DIM:], ls)
            lses.append(ms * SCALE2 + jnp.log2(ls))
            if b == 0:
                if f == 0 and kv > 1:
                    forward(1, n - 1)
                elif f > 0:
                    for h in range(2, n - 1):
                        stage(f - 1, h)
        put_s = jnp.dot(
            place_f,
            jnp.concatenate(lses, axis=0),
            precision=lax.Precision.HIGHEST,
            preferred_element_type=jnp.float32,
        )
        put_s = jnp.where(held > 0.5, put_s, MASKED)
        root_sum = root_l[...]
        root_lse = root_m[...] * SCALE2 + jnp.log2(root_sum)
        top = jnp.maximum(root_lse, put_s)
        root_w = jnp.exp2(root_lse - top)
        branch_w = jnp.exp2(put_s - top)
        total = root_w + branch_w
        joined = split(top + jnp.log2(total), all_lane)
        root_m[...] = root_w / (total * root_sum)
        root_l[...] = branch_w / total
        for s in range(n):
            part[f, s, :, side_cols] = joined[s * rows : (s + 1) * rows]
        put_o = jnp.dot(place_b, branch_o[...], preferred_element_type=jnp.float32)
        for h in range(GROUP):
            cols = slice(h * HEAD_DIM, (h + 1) * HEAD_DIM)
            mixed = (
                root_o[:, cols] * root_m[:, h : h + 1] + put_o[:, cols] * root_l[:, h : h + 1]
            ).astype(jnp.bfloat16)
            for s in range(n):
                part[f, s, :, cols] = mixed[s * rows : (s + 1) * rows]
        stage(f, 0)
        if f > 0:
            finish(f - 1)
    for h in range(1, n - 1):
        stage(kv - 1, h)
    finish(kv - 1)

    for f in range(kv):
        for hop in range(n - 1):
            sent(f, hop)
        for k in range(1, n):
            p_copy(f, lax.rem(me + k, n), 0).wait_send()


def body(n, queries, root_keys, root_values, branch_keys, branch_values, branch_id, doc_len):
    rows = queries.shape[0]
    kv = root_keys.shape[1] // HEAD_DIM
    root_len = root_keys.shape[0]
    branches, branch_len = branch_keys.shape[:2]
    width = GROUP * HEAD_DIM
    all_rows = n * rows
    most = 2 * rows // branches
    slots = branches * most
    any_spec = pl.BlockSpec(memory_space=pl.ANY)
    bf16, f32 = jnp.bfloat16, jnp.float32
    dma = pltpu.SemaphoreType.DMA
    return pl.pallas_call(
        functools.partial(kernel, n, kv),
        out_shape=jax.ShapeDtypeStruct(queries.shape, bf16),
        in_specs=[any_spec] * 5
        + [pl.BlockSpec(memory_space=pltpu.VMEM), pl.BlockSpec(memory_space=pltpu.SMEM)],
        out_specs=pl.BlockSpec(memory_space=pltpu.VMEM),
        scratch_shapes=[
            pltpu.VMEM((kv, all_rows, width), bf16),
            pltpu.VMEM((kv, root_len, HEAD_DIM), bf16),
            pltpu.VMEM((kv, root_len, 2 * HEAD_DIM), bf16),
            pltpu.VMEM((kv, branches, branch_len, HEAD_DIM), bf16),
            pltpu.VMEM((kv, branches, branch_len, 2 * HEAD_DIM), bf16),
            pltpu.VMEM((all_rows, width), f32),
            pltpu.VMEM((all_rows, HEAD_DIM), f32),
            pltpu.VMEM((all_rows, HEAD_DIM), f32),
            pltpu.VMEM((slots, width), bf16),
            pltpu.VMEM((kv, n, rows, width + HEAD_DIM), bf16),
            pltpu.VMEM((kv, n, 2, rows, width + HEAD_DIM), bf16),
            dma((kv,)),
            dma((4, kv, branches)),
            dma((kv, 2, n)),
            dma((kv, n)),
            dma((kv, n)),
            dma((kv, n, 2)),
        ],
        compiler_params=pltpu.CompilerParams(
            collective_id=0, has_side_effects=True, vmem_limit_bytes=60 * 1024 * 1024
        ),
    )(queries, root_keys, root_values, branch_keys, branch_values, branch_id.reshape(1, -1), doc_len)


def solution(mesh):
    in_specs = (
        P(("parts", "seq"), "head"),
        P(("parts", "seq"), "head"),
        P(("parts", "seq"), "head"),
        P(("parts", "seq"), None, "head"),
        P(("parts", "seq"), None, "head"),
        P("parts", None),
        P("parts"),
    )
    out_specs = P(("parts", "seq"), "head")
    return jax.shard_map(
        functools.partial(body, mesh.shape["seq"]),
        mesh=mesh,
        in_specs=in_specs,
        out_specs=out_specs,
        check_vma=False,
    )
```

```python
import functools

import jax
import jax.numpy as jnp
from jax import lax
from jax.experimental import pallas as pl
from jax.experimental.pallas import tpu as pltpu
from jax.sharding import PartitionSpec as P

QHEADS = 64
KVHEADS = 8
HEAD_DIM = 128
GROUP = QHEADS // KVHEADS
MESH = pl.DeviceIdType.MESH
LOG2E = 1.4426950408889634
SCALE2 = HEAD_DIM ** (-0.5) * LOG2E
MASKED = -1e30
KEY_BLOCK = 512


def attend(q, keys, values, live=None):
    size = min(KEY_BLOCK, keys.shape[0])
    blocks = [slice(i, i + size) for i in range(0, keys.shape[0], size)]
    scores = []
    for block in blocks:
        s = lax.dot_general(
            q, keys[block], (((1,), (1,)), ((), ())), preferred_element_type=jnp.float32
        )
        if live is not None:
            s = jnp.where(live[:, block], s, MASKED)
        scores.append(s)
    tops, sums = [], []
    for block, s in zip(blocks, scores):
        t = jnp.max(s, axis=1, keepdims=True)
        p = jnp.exp2((s - t) * SCALE2).astype(jnp.bfloat16)
        tops.append(t)
        sums.append(jnp.dot(p, values[block], preferred_element_type=jnp.float32))
    m = functools.reduce(jnp.maximum, tops)
    o = functools.reduce(
        jnp.add, [x * jnp.exp2((t - m) * SCALE2) for x, t in zip(sums, tops)]
    )
    return m, o


def stack_heads(rows):
    return jnp.concatenate(
        [rows[:, h * HEAD_DIM : (h + 1) * HEAD_DIM] for h in range(GROUP)], axis=0
    )


def kernel(
    n,
    kv,
    q_hbm,
    rk_hbm,
    rv_hbm,
    bk_hbm,
    bv_hbm,
    id_ref,
    len_ref,
    out_ref,
    qg,
    rk,
    rv,
    bk,
    bv,
    root_o,
    root_m,
    root_l,
    branch_o,
    part,
    recv,
    own_sem,
    load_sem,
    qsend_sem,
    qrecv_sem,
    psend_sem,
    precv_sem,
):
    me = lax.axis_index("seq")
    rows = q_hbm.shape[0]
    all_rows = n * rows
    width = GROUP * HEAD_DIM
    branches = bk_hbm.shape[0]
    branch_len = bk_hbm.shape[1]
    most = 2 * rows // branches
    slots = branches * most
    has_left, has_right = me > 0, me < n - 1

    barrier = pltpu.get_barrier_semaphore()

    @pl.when(has_left)
    def _():
        pl.semaphore_signal(barrier, inc=1, device_id={"seq": me - 1}, device_id_type=MESH)

    @pl.when(has_right)
    def _():
        pl.semaphore_signal(barrier, inc=1, device_id={"seq": me + 1}, device_id_type=MESH)

    def head_cols(f):
        return pl.ds(f * HEAD_DIM, HEAD_DIM)

    def shard_rows(s):
        return pl.ds(pl.multiple_of(s * rows, rows), rows)

    own, loads_k, loads_v = [], [], []
    for f in range(kv):
        own.append(
            pltpu.make_async_copy(
                q_hbm.at[:, pl.ds(f * width, width)], qg.at[f, shard_rows(me)], own_sem.at[f]
            )
        )
        loads_k.append(
            pltpu.make_async_copy(rk_hbm.at[:, head_cols(f)], rk.at[f], load_sem.at[0, f, 0])
        )
        loads_v.append(
            pltpu.make_async_copy(
                rv_hbm.at[:, head_cols(f)], rv.at[f, :, pl.ds(0, HEAD_DIM)], load_sem.at[1, f, 0]
            )
        )
    bloads_k, bloads_v = [], []
    for f in range(kv):
        bloads_k.append(
            [
                pltpu.make_async_copy(
                    bk_hbm.at[b, :, head_cols(f)], bk.at[f, b], load_sem.at[2, f, b]
                )
                for b in range(branches)
            ]
        )
        bloads_v.append(
            [
                pltpu.make_async_copy(
                    bv_hbm.at[b, :, head_cols(f)],
                    bv.at[f, b, :, pl.ds(0, HEAD_DIM)],
                    load_sem.at[3, f, b],
                )
                for b in range(branches)
            ]
        )
    own[0].start()
    loads_k[0].start()

    for f in range(kv):
        rv[f, :, HEAD_DIM:] = jnp.ones((rv.shape[1], HEAD_DIM), jnp.bfloat16)
        loads_v[f].start()
        if f:
            loads_k[f].start()
            own[f].start()
        for b in range(branches):
            bv[f, b, :, HEAD_DIM:] = jnp.ones((branch_len, HEAD_DIM), jnp.bfloat16)
            bloads_k[f][b].start()
            bloads_v[f][b].start()

    pl.semaphore_wait(barrier, jnp.where(has_left & has_right, 2, 1))

    def q_copy(f, s, way, hop, src):
        return pltpu.make_async_remote_copy(
            src_ref=src,
            dst_ref=qg.at[f, shard_rows(s)],
            send_sem=qsend_sem.at[f, way, hop],
            recv_sem=qrecv_sem.at[f, s],
            device_id={"seq": me + 1 if way == 0 else me - 1},
            device_id_type=MESH,
        )

    def send_own(f):
        src = q_hbm.at[:, pl.ds(f * width, width)]

        @pl.when(has_right)
        def _():
            q_copy(f, me, 0, 0, src).start()

        @pl.when(has_left)
        def _():
            q_copy(f, me, 1, 0, src).start()

    def pass_right(f, hop):
        s = me - hop
        block = qg.at[f, shard_rows(s)]
        q_copy(f, s, 0, hop, block).wait_recv()

        @pl.when(has_right)
        def _():
            q_copy(f, s, 0, hop, block).start()

    def pass_left(f, hop):
        s = me + hop
        block = qg.at[f, shard_rows(s)]
        q_copy(f, s, 1, hop, block).wait_recv()

        @pl.when(has_left)
        def _():
            q_copy(f, s, 1, hop, block).start()

    def forward(f, hop):
        @pl.when(me - hop >= 0)
        def _():
            pass_right(f, hop)

        @pl.when(me + hop < n)
        def _():
            pass_left(f, hop)

    def sent(f, hop):
        left, right = me - hop, me + hop

        @pl.when((left >= 0) & has_right)
        def _():
            q_copy(f, left, 0, hop, qg.at[f, shard_rows(left)]).wait_send()

        @pl.when((right < n) & has_left)
        def _():
            q_copy(f, right, 1, hop, qg.at[f, shard_rows(right)]).wait_send()

    send_own(0)

    slot = lax.broadcasted_iota(jnp.int32, (slots, all_rows), 0)
    named = id_ref[...] == me * branches + slot // most
    named_b = jnp.where(named, 1.0, 0.0).astype(jnp.bfloat16)
    tri = jnp.where(
        lax.broadcasted_iota(jnp.int32, (all_rows, all_rows), 0)
        <= lax.broadcasted_iota(jnp.int32, (all_rows, all_rows), 1),
        1.0,
        0.0,
    ).astype(jnp.bfloat16)
    rank = jnp.dot(named_b, tri, preferred_element_type=jnp.float32)
    pick_f = jnp.where(named & (rank == (lax.rem(slot, most) + 1).astype(jnp.float32)), 1.0, 0.0)
    pick_b = pick_f.astype(jnp.bfloat16)
    place_f = pick_f.T
    place_b = place_f.astype(jnp.bfloat16)
    held = jnp.dot(
        place_b, jnp.ones((slots, HEAD_DIM), jnp.bfloat16), preferred_element_type=jnp.float32
    )

    lane = lax.broadcasted_iota(jnp.int32, (rows, HEAD_DIM), 1)
    all_lane = lax.broadcasted_iota(jnp.int32, (all_rows, HEAD_DIM), 1)
    slot_lane = lax.broadcasted_iota(jnp.int32, (most, HEAD_DIM), 1)
    position = lax.broadcasted_iota(jnp.int32, (1, branch_len), 1)
    side_cols = slice(width, width + HEAD_DIM)

    def split(x, lanes):
        high = x.astype(jnp.bfloat16).astype(jnp.float32)
        rest = x - high
        mid = rest.astype(jnp.bfloat16).astype(jnp.float32)
        low = rest - mid
        return jnp.where(
            lanes < GROUP,
            high,
            jnp.where(
                lanes < 2 * GROUP, pltpu.roll(mid, GROUP, axis=1), pltpu.roll(low, 2 * GROUP, axis=1)
            ),
        ).astype(jnp.bfloat16)

    def whole(x):
        x = x.astype(jnp.float32)
        return (
            x
            + pltpu.roll(x, HEAD_DIM - GROUP, axis=1)
            + pltpu.roll(x, HEAD_DIM - 2 * GROUP, axis=1)
        )

    def a_copy(f, d, src):
        return pltpu.make_async_remote_copy(
            src_ref=part.at[f, d],
            dst_ref=recv.at[f, src],
            send_sem=psend_sem.at[f, d],
            recv_sem=precv_sem.at[f, src],
            device_id={"seq": d},
            device_id_type=MESH,
        )

    def send(f):
        for k in range(1, n):
            a_copy(f, lax.rem(me + k, n), me).start()

    def finish(f):
        for k in range(1, n):
            a_copy(f, me, lax.rem(me + k, n)).wait_recv()
        recv[f, me] = part[f, me]
        lse = [whole(recv[f, s, :, side_cols]) for s in range(n)]
        top = functools.reduce(jnp.maximum, lse)
        weights = [jnp.exp2(x - top) for x in lse]
        total = functools.reduce(jnp.add, weights)
        coefs = [w / total for w in weights]
        for h in range(GROUP):
            cols = slice(h * HEAD_DIM, (h + 1) * HEAD_DIM)
            acc = recv[f, 0, :, cols].astype(jnp.float32) * coefs[0][:, h : h + 1]
            for s in range(1, n):
                acc += recv[f, s, :, cols].astype(jnp.float32) * coefs[s][:, h : h + 1]
            out_ref[:, f * width + h * HEAD_DIM : f * width + (h + 1) * HEAD_DIM] = acc.astype(jnp.bfloat16)

    def root(f, s):
        m, o = attend(stack_heads(qg[f, shard_rows(s)]), rk[f], rv[f])
        ms = jnp.zeros((rows, HEAD_DIM), jnp.float32)
        ls = jnp.ones((rows, HEAD_DIM), jnp.float32)
        for h in range(GROUP):
            block = slice(h * rows, (h + 1) * rows)
            root_o[shard_rows(s), h * HEAD_DIM : (h + 1) * HEAD_DIM] = o[block, :HEAD_DIM]
            ms = jnp.where(lane == h, m[block], ms)
            ls = jnp.where(lane == h, o[block, HEAD_DIM:], ls)
        root_m[shard_rows(s)] = ms
        root_l[shard_rows(s)] = ls

    own[0].wait()
    loads_k[0].wait()
    loads_v[0].wait()

    for f in range(kv):
        if f == 0:

            def first_step(j, carry):
                hop, left = (j + 1) // 2, lax.rem(j, 2) == 1
                s = jnp.where(left, me - hop, me + hop)

                @pl.when(left & (s >= 0))
                def _():
                    pass_right(0, hop)

                @pl.when((j > 0) & jnp.logical_not(left) & (s < n))
                def _():
                    pass_left(0, hop)

                if kv > 1:

                    @pl.when(j == 2)
                    def _():
                        send_own(1)

                    @pl.when((j > 2) & jnp.logical_not(left))
                    def _():
                        forward(1, hop - 1)

                @pl.when((s >= 0) & (s < n))
                def _():
                    root(0, s)

                return carry

            lax.fori_loop(0, 2 * n - 1, first_step, 0)
        else:
            own[f].wait()
            loads_k[f].wait()
            loads_v[f].wait()

            def root_step(s, carry, f=f):
                root(f, s)
                return carry

            lax.fori_loop(0, n, root_step, 0)

        picked = jnp.dot(pick_b, qg[f], preferred_element_type=jnp.float32).astype(jnp.bfloat16)
        lses = []
        for b in range(branches):
            bloads_k[f][b].wait()
            bloads_v[f][b].wait()
            live = position < len_ref[me * branches + b]
            m, o = attend(
                stack_heads(picked[b * most : (b + 1) * most]), bk[f, b], bv[f, b], live
            )
            ms = jnp.zeros((most, HEAD_DIM), jnp.float32)
            ls = jnp.ones((most, HEAD_DIM), jnp.float32)
            for h in range(GROUP):
                block = slice(h * most, (h + 1) * most)
                branch_o[b * most : (b + 1) * most, h * HEAD_DIM : (h + 1) * HEAD_DIM] = (
                    o[block, :HEAD_DIM] / o[block, HEAD_DIM:]
                ).astype(jnp.bfloat16)
                ms = jnp.where(slot_lane == h, m[block], ms)
                ls = jnp.where(slot_lane == h, o[block, HEAD_DIM:], ls)
            lses.append(ms * SCALE2 + jnp.log2(ls))
            if b == 0:
                if f == 0 and kv > 1:
                    forward(1, n - 1)
        put_s = jnp.dot(
            place_f,
            jnp.concatenate(lses, axis=0),
            precision=lax.Precision.HIGHEST,
            preferred_element_type=jnp.float32,
        )
        put_s = jnp.where(held > 0.5, put_s, MASKED)
        root_sum = root_l[...]
        root_lse = root_m[...] * SCALE2 + jnp.log2(root_sum)
        top = jnp.maximum(root_lse, put_s)
        root_w = jnp.exp2(root_lse - top)
        branch_w = jnp.exp2(put_s - top)
        total = root_w + branch_w
        joined = split(top + jnp.log2(total), all_lane)
        root_m[...] = root_w / (total * root_sum)
        root_l[...] = branch_w / total
        for s in range(n):
            part[f, s, :, side_cols] = joined[s * rows : (s + 1) * rows]
        put_o = jnp.dot(place_b, branch_o[...], preferred_element_type=jnp.float32)
        for h in range(GROUP):
            cols = slice(h * HEAD_DIM, (h + 1) * HEAD_DIM)
            mixed = (
                root_o[:, cols] * root_m[:, h : h + 1] + put_o[:, cols] * root_l[:, h : h + 1]
            ).astype(jnp.bfloat16)
            for s in range(n):
                part[f, s, :, cols] = mixed[s * rows : (s + 1) * rows]
        send(f)
        if f > 0:
            finish(f - 1)
    finish(kv - 1)

    for f in range(kv):
        for hop in range(n - 1):
            sent(f, hop)
        for k in range(1, n):
            a_copy(f, lax.rem(me + k, n), me).wait_send()


def body(n, queries, root_keys, root_values, branch_keys, branch_values, branch_id, doc_len):
    rows = queries.shape[0]
    kv = root_keys.shape[1] // HEAD_DIM
    root_len = root_keys.shape[0]
    branches, branch_len = branch_keys.shape[:2]
    width = GROUP * HEAD_DIM
    all_rows = n * rows
    most = 2 * rows // branches
    slots = branches * most
    any_spec = pl.BlockSpec(memory_space=pl.ANY)
    bf16, f32 = jnp.bfloat16, jnp.float32
    dma = pltpu.SemaphoreType.DMA
    return pl.pallas_call(
        functools.partial(kernel, n, kv),
        out_shape=jax.ShapeDtypeStruct(queries.shape, bf16),
        in_specs=[any_spec] * 5
        + [pl.BlockSpec(memory_space=pltpu.VMEM), pl.BlockSpec(memory_space=pltpu.SMEM)],
        out_specs=pl.BlockSpec(memory_space=pltpu.VMEM),
        scratch_shapes=[
            pltpu.VMEM((kv, all_rows, width), bf16),
            pltpu.VMEM((kv, root_len, HEAD_DIM), bf16),
            pltpu.VMEM((kv, root_len, 2 * HEAD_DIM), bf16),
            pltpu.VMEM((kv, branches, branch_len, HEAD_DIM), bf16),
            pltpu.VMEM((kv, branches, branch_len, 2 * HEAD_DIM), bf16),
            pltpu.VMEM((all_rows, width), f32),
            pltpu.VMEM((all_rows, HEAD_DIM), f32),
            pltpu.VMEM((all_rows, HEAD_DIM), f32),
            pltpu.VMEM((slots, width), bf16),
            pltpu.VMEM((kv, n, rows, width + HEAD_DIM), bf16),
            pltpu.VMEM((kv, n, rows, width + HEAD_DIM), bf16),
            dma((kv,)),
            dma((4, kv, branches)),
            dma((kv, 2, n)),
            dma((kv, n)),
            dma((kv, n)),
            dma((kv, n)),
        ],
        compiler_params=pltpu.CompilerParams(
            collective_id=0, has_side_effects=True, vmem_limit_bytes=60 * 1024 * 1024
        ),
    )(queries, root_keys, root_values, branch_keys, branch_values, branch_id.reshape(1, -1), doc_len)


def solution(mesh):
    in_specs = (
        P(("parts", "seq"), "head"),
        P(("parts", "seq"), "head"),
        P(("parts", "seq"), "head"),
        P(("parts", "seq"), None, "head"),
        P(("parts", "seq"), None, "head"),
        P("parts", None),
        P("parts"),
    )
    out_specs = P(("parts", "seq"), "head")
    return jax.shard_map(
        functools.partial(body, mesh.shape["seq"]),
        mesh=mesh,
        in_specs=in_specs,
        out_specs=out_specs,
        check_vma=False,
    )
```
